256 devices in a mesh: seq: 32 (over x, z), head: 8 (over y, core).
Axes of the slice: x: 4, y: 4, z: 8, core: 2. Of those that a mesh axis runs over, the one named last changes fastest.
Arguments:
- cached_probs: bfloat16 [128, 40, 8, 128, 128], P('seq', 'head'), may hold values from 0 to 1, as said below
- out_old: bfloat16 [16384, 5120], P('seq', 'head'), may hold values from -6 to 6
- key_lists: int32 [128, 8], P('seq'), may hold values from 0 to 127, as said below
- changed_block_numbers: int32 [32], replicated, may hold values from 0 to 127, as said below
- delta_v: bfloat16 [4096, 1024], P('seq', 'head'), may hold values from -24 to 24
- w_out: bfloat16 [5120, 5120], P('head', 'seq'), may hold values from -0.078125 to 0.078125
Outputs:
- attn_new: bfloat16 [16384, 5120], P('seq', 'head')
- out_proj: bfloat16 [16384, 5120], P('seq', 'head')
The draws below stay inside these ranges and needn't reach their ends.
Inputs may be any that keep to these rules, and one draw needn't show every extreme that they name: `changed_block_numbers`: the changed block numbers are all different; the first block and the last block are always among them. `key_lists`: each query block lists 8 different key blocks; some list many changed blocks, most list few. `cached_probs`: for each query block, head and row, the weights over the row's listed keys are positive and sum to at most 1.
All inputs are finite; a program needn't handle non-finite values.
Results may differ from the reference program's by a relative error of at most 0.017.
Values may be sent and summed in bfloat16 or wider, within the bound.
A program may use at most 128 MiB of HBM per device.

```python
import jax
import jax.numpy as jnp
from jax import lax

D = 5120
HQ = 40
KVH = 8
HD = 128
BLK = 128
TOP_KEY_BLOCKS = 8
GROUP = 5
HQ_DEV = 5
TOKENS = 16384
NB = 128
NCB = 32
N_HEAD = 8


def pick_changed(key):
    middle = jax.random.permutation(jax.random.fold_in(key, 11), NB - 2)[:NCB - 2].astype(jnp.int32) + 1
    ends = jnp.array([0, NB - 1], jnp.int32)
    chosen = jnp.concatenate([ends, middle])
    return jax.random.permutation(jax.random.fold_in(key, 12), chosen).astype(jnp.int32)


def draw_changed_block_numbers(key, part):
    return pick_changed(key)


def draw_cached_probs(key, part):
    block_keys = jax.random.split(jax.random.fold_in(key, 31), NB)

    def one_block(block_key):
        logit_key, share_key = jax.random.split(block_key, 2)
        logits = 2.5 * jax.random.normal(logit_key, (HQ, TOP_KEY_BLOCKS, BLK, BLK), jnp.float32)
        weights = jax.nn.softmax(logits, axis=(1, 3))
        share = jax.random.uniform(share_key, (HQ, 1, BLK, 1), jnp.float32, 0.5, 1.0)
        return (weights * share).astype(jnp.bfloat16)
    return lax.map(one_block, block_keys)


def draw_key_lists(key, part):
    changed = pick_changed(key)
    marked = jnp.zeros((NB,), jnp.int32).at[changed].set(1)
    ordered = jnp.argsort(marked, stable=True).astype(jnp.int32)
    unchanged = ordered[:NB - NCB]
    row_keys = jax.random.split(jax.random.fold_in(key, 23), NB)

    def one_row(row_key):
        partition_keys = jax.random.split(row_key, 6)
        baseline_count = jax.random.randint(partition_keys[0], (), 0, 3)
        spike_enabled = (jax.random.randint(partition_keys[1], (), 0, 4) == 0).astype(jnp.int32)
        spike_count = spike_enabled * jax.random.randint(partition_keys[2], (), 0, TOP_KEY_BLOCKS + 1)
        total_count = jnp.minimum(baseline_count + spike_count, TOP_KEY_BLOCKS)
        from_changed = jax.random.permutation(partition_keys[3], changed)[:TOP_KEY_BLOCKS]
        from_rest = jax.random.permutation(partition_keys[4], unchanged)[:TOP_KEY_BLOCKS]
        slots = jnp.arange(TOP_KEY_BLOCKS, dtype=jnp.int32)
        merged = jnp.where(slots < total_count, from_changed, from_rest)
        return jax.random.permutation(partition_keys[5], merged)
    return jax.vmap(one_row)(row_keys).astype(jnp.int32)


def steps_of(own_key, extent, shards, low, top_value):
    def one(axis_at, blocks):
        steps = jax.random.uniform(jax.random.fold_in(jax.random.fold_in(own_key, 6), axis_at), (blocks,), jnp.float32, low / len(shards), top_value / len(shards))
        return jnp.repeat(jnp.exp(steps), extent[axis_at] // blocks).reshape((-1,) + (1,) * (len(extent) - axis_at - 1))

    level = one(*shards[0])
    for cut in shards[1:]:
        level = level * one(*cut)
    return level


def scatter_about(stream_key, shape, deviation, limit, pieces=(), kind=jnp.bfloat16):
    values = jax.random.normal(stream_key, shape, jnp.float32) * deviation
    if len(pieces) > 0:
        values = steps_of(stream_key, shape, pieces, -0.22, 0.18) * values
    return jnp.clip(values, min=-limit, max=limit).astype(kind)


def setup_inputs(seed: int = 0) -> dict:
    seeds = jax.random.split(jax.random.key(seed), 7)
    return {
        "cached_probs": draw_cached_probs(jax.random.fold_in(seeds[6], 71), 0),
        "out_old": scatter_about(seeds[1], (TOKENS, HQ * HD), 1.0, 6.0, ((0, 32), (1, 8))),
        "key_lists": draw_key_lists(jax.random.fold_in(seeds[6], 71), 0),
        "changed_block_numbers": draw_changed_block_numbers(jax.random.fold_in(seeds[6], 71), 0),
        "delta_v": scatter_about(seeds[4], (NCB * BLK, KVH * HD), 4.0, 24.0, ((0, 32), (1, 8))),
        "w_out": scatter_about(seeds[5], (HQ * HD, D), (HQ * HD) ** -0.5, 0.078125, ((0, 8), (1, 32))),
    }


def reference(cached_probs, out_old, key_lists, changed_block_numbers, delta_v, w_out):
    changes_f = delta_v.reshape(NCB, BLK * KVH * HD).astype(jnp.float32)

    def one_block(inputs):
        prob_tiles, block_listing = inputs
        onehot = (block_listing[:, None] == changed_block_numbers[None, :]).astype(jnp.float32)
        picked = jnp.dot(onehot, changes_f).astype(jnp.bfloat16)
        picked = picked.reshape(TOP_KEY_BLOCKS, BLK, KVH, HD).astype(jnp.float32)
        weights = prob_tiles.astype(jnp.float32).reshape(KVH, GROUP, TOP_KEY_BLOCKS, BLK, BLK)
        result = jnp.einsum("vgkij,kjvd->ivgd", weights, picked)
        return result.reshape(BLK, HQ * HD)

    delta_out = lax.map(one_block, (cached_probs, key_lists)).reshape(TOKENS, HQ * HD)
    attn_new = (out_old.astype(jnp.float32) + delta_out).astype(jnp.bfloat16)
    width = HQ_DEV * HD
    summed = jnp.zeros((TOKENS, D), jnp.float32)
    for group in range(N_HEAD):
        partial_value = jnp.dot(attn_new[:, group * width:(group + 1) * width], w_out[group * width:(group + 1) * width, :], preferred_element_type=jnp.float32).astype(jnp.bfloat16)
        partial_value = lax.optimization_barrier(partial_value)
        summed = summed + partial_value.astype(jnp.float32)
    return attn_new, summed.astype(jnp.bfloat16)
```

```python
import jax
import jax.numpy as jnp
from jax import lax
from jax.experimental import pallas as pl
from jax.experimental.pallas import tpu as pltpu
from jax.sharding import PartitionSpec as P

HD = 128
BLK = 128
GROUP = 5


def _gather_kernel(n, x_ref, o_ref, send_sem, recv_sem, local_sem):
    me = lax.axis_index("seq")
    hh = lax.axis_index("head")
    own = pltpu.make_async_copy(x_ref, o_ref.at[me], local_sem)
    own.start()
    copies = []
    for k in range(1, n):
        peer = lax.rem(me + k, n)
        copy = pltpu.make_async_remote_copy(
            src_ref=x_ref,
            dst_ref=o_ref.at[me],
            send_sem=send_sem.at[k],
            recv_sem=recv_sem.at[k],
            device_id=(peer, hh),
            device_id_type=pl.DeviceIdType.MESH,
        )
        copy.start()
        copies.append(copy)
    for copy in copies:
        copy.wait_send()
    for copy in copies:
        copy.wait_recv()
    own.wait()


def gather_seq(x, n):
    return pl.pallas_call(
        lambda *refs: _gather_kernel(n, *refs),
        out_shape=jax.ShapeDtypeStruct((n,) + x.shape, x.dtype),
        in_specs=[pl.BlockSpec(memory_space=pl.ANY)],
        out_specs=pl.BlockSpec(memory_space=pl.ANY),
        scratch_shapes=[
            pltpu.SemaphoreType.DMA((n,)),
            pltpu.SemaphoreType.DMA((n,)),
            pltpu.SemaphoreType.DMA,
        ],
        compiler_params=pltpu.CompilerParams(has_side_effects=True),
    )(x)


def local(n_seq, cached_probs, out_old, key_lists, changed_block_numbers, delta_v, w_out):
    blocks_here = cached_probs.shape[0]
    heads_here = cached_probs.shape[1]
    topk_here = cached_probs.shape[2]
    values_here = heads_here // GROUP
    w_full = lax.all_gather(w_out, "seq", axis=1, tiled=True)
    every_change = gather_seq(delta_v, n_seq)
    every_change = every_change.reshape(n_seq * delta_v.shape[0] // BLK, BLK * values_here * HD)
    flat_lists = key_lists.reshape(blocks_here * topk_here)
    onehot = (flat_lists[:, None] == changed_block_numbers[None, :]).astype(jnp.bfloat16)
    selected = jnp.dot(onehot, every_change, preferred_element_type=jnp.float32)
    picked = selected.astype(jnp.bfloat16).reshape(blocks_here, topk_here, BLK, values_here, HD)
    tiles = cached_probs.reshape(blocks_here, values_here, GROUP, topk_here, BLK, BLK)
    delta_out = jnp.einsum("qvgkij,qkjvd->qivgd", tiles, picked, preferred_element_type=jnp.float32)
    delta_out = delta_out.reshape(blocks_here * BLK, heads_here * HD)
    attn_new = (out_old.astype(jnp.float32) + delta_out).astype(jnp.bfloat16)
    terms = jnp.dot(attn_new, w_full, preferred_element_type=jnp.float32)
    out_proj = lax.psum_scatter(terms.astype(jnp.bfloat16), "head", scatter_dimension=1, tiled=True)
    return (attn_new, out_proj)


def solution(mesh):
    placed = (
        P("seq", "head", None, None, None),
        P("seq", "head"),
        P("seq", None),
        P(),
        P("seq", "head"),
        P("head", "seq"),
    )
    n_seq = mesh.shape["seq"]
    return jax.shard_map(
        lambda *a: local(n_seq, *a),
        mesh=mesh,
        in_specs=placed,
        out_specs=(P("seq", "head"), P("seq", "head")),
        check_vma=False,
    )
```

```python
import jax
import jax.numpy as jnp
from jax import lax
from jax.experimental import pallas as pl
from jax.experimental.pallas import tpu as pltpu
from jax.sharding import PartitionSpec as P

HD = 128
BLK = 128
GROUP = 5


def _gather_kernel(n, x_ref, o_ref, send_sem, recv_sem, local_sem):
    me = lax.axis_index("seq")
    hh = lax.axis_index("head")
    own = pltpu.make_async_copy(x_ref, o_ref.at[me], local_sem)
    own.start()
    copies = []
    for k in range(1, n):
        peer = lax.rem(me + k, n)
        copy = pltpu.make_async_remote_copy(
            src_ref=x_ref,
            dst_ref=o_ref.at[me],
            send_sem=send_sem.at[k],
            recv_sem=recv_sem.at[k],
            device_id=(peer, hh),
            device_id_type=pl.DeviceIdType.MESH,
        )
        copy.start()
        copies.append(copy)
    for copy in copies:
        copy.wait_send()
    for copy in copies:
        copy.wait_recv()
    own.wait()


def gather_seq(x, n):
    return pl.pallas_call(
        lambda *refs: _gather_kernel(n, *refs),
        out_shape=jax.ShapeDtypeStruct((n,) + x.shape, x.dtype),
        in_specs=[pl.BlockSpec(memory_space=pl.ANY)],
        out_specs=pl.BlockSpec(memory_space=pl.ANY),
        scratch_shapes=[
            pltpu.SemaphoreType.DMA((n,)),
            pltpu.SemaphoreType.DMA((n,)),
            pltpu.SemaphoreType.DMA,
        ],
        compiler_params=pltpu.CompilerParams(has_side_effects=True),
    )(x)


def local(n_seq, cached_probs, out_old, key_lists, changed_block_numbers, delta_v, w_out):
    blocks_here = cached_probs.shape[0]
    heads_here = cached_probs.shape[1]
    topk_here = cached_probs.shape[2]
    values_here = heads_here // GROUP
    w_full = lax.all_gather(w_out, "seq", axis=1, tiled=True)
    every_change = gather_seq(delta_v, n_seq)
    every_change = every_change.reshape(n_seq * delta_v.shape[0] // BLK, BLK * values_here * HD)
    flat_lists = key_lists.reshape(blocks_here * topk_here)
    onehot = (flat_lists[:, None] == changed_block_numbers[None, :]).astype(jnp.bfloat16)
    selected = jnp.dot(onehot, every_change, preferred_element_type=jnp.float32)
    picked = selected.astype(jnp.bfloat16).reshape(blocks_here, topk_here, BLK, values_here, HD)
    tiles = cached_probs.reshape(blocks_here, values_here, GROUP, topk_here, BLK, BLK)
    delta_out = jnp.einsum("qvgkij,qkjvd->qivgd", tiles, picked, preferred_element_type=jnp.float32)
    delta_out = delta_out.reshape(blocks_here * BLK, heads_here * HD)
    attn_new = (out_old.astype(jnp.float32) + delta_out).astype(jnp.bfloat16)
    n_head = w_full.shape[1] // attn_new.shape[1]
    w_groups = w_full.reshape(w_full.shape[0], n_head, attn_new.shape[1])
    terms = jnp.einsum("tk,kgc->gtc", attn_new, w_groups, preferred_element_type=jnp.float32)
    out_proj = lax.psum_scatter(terms.astype(jnp.bfloat16), "head", scatter_dimension=0, tiled=True)[0]
    return (attn_new, out_proj)


def solution(mesh):
    placed = (
        P("seq", "head", None, None, None),
        P("seq", "head"),
        P("seq", None),
        P(),
        P("seq", "head"),
        P("head", "seq"),
    )
    n_seq = mesh.shape["seq"]
    return jax.shard_map(
        lambda *a: local(n_seq, *a),
        mesh=mesh,
        in_specs=placed,
        out_specs=(P("seq", "head"), P("seq", "head")),
        check_vma=False,
    )
```

```python
import jax
import jax.numpy as jnp
from jax import lax
from jax.experimental import pallas as pl
from jax.experimental.pallas import tpu as pltpu
from jax.sharding import PartitionSpec as P

HD = 128
BLK = 128
GROUP = 5


def _gather_kernel(n, x_ref, o_ref, send_sem, recv_sem, local_sem):
    me = lax.axis_index("seq")
    hh = lax.axis_index("head")
    own = pltpu.make_async_copy(x_ref, o_ref.at[me], local_sem)
    own.start()
    copies = []
    for k in range(1, n):
        peer = lax.rem(me + k, n)
        copy = pltpu.make_async_remote_copy(
            src_ref=x_ref,
            dst_ref=o_ref.at[me],
            send_sem=send_sem.at[k],
            recv_sem=recv_sem.at[k],
            device_id=(peer, hh),
            device_id_type=pl.DeviceIdType.MESH,
        )
        copy.start()
        copies.append(copy)
    for copy in copies:
        copy.wait_send()
    for copy in copies:
        copy.wait_recv()
    own.wait()


def gather_seq(x, n):
    return pl.pallas_call(
        lambda *refs: _gather_kernel(n, *refs),
        out_shape=jax.ShapeDtypeStruct((n,) + x.shape, x.dtype),
        in_specs=[pl.BlockSpec(memory_space=pl.ANY)],
        out_specs=pl.BlockSpec(memory_space=pl.ANY),
        scratch_shapes=[
            pltpu.SemaphoreType.DMA((n,)),
            pltpu.SemaphoreType.DMA((n,)),
            pltpu.SemaphoreType.DMA,
        ],
        compiler_params=pltpu.CompilerParams(has_side_effects=True),
    )(x)


def ring_reduce_scatter(attn_new, w_full):
    n = w_full.shape[1] // attn_new.shape[1]
    width = attn_new.shape[1]
    rows = attn_new.shape[0]
    half = rows // 2
    me = lax.axis_index("head")
    halves = (attn_new[:half], attn_new[half:])
    shifts = (1, n - 1)

    def partial(which, group):
        cols = lax.dynamic_slice_in_dim(w_full, group * width, width, axis=1)
        term = jnp.dot(halves[which], cols, preferred_element_type=jnp.float32)
        return term.astype(jnp.bfloat16).astype(jnp.float32)

    accs = []
    for which in range(2):
        sign = 1 if which == 0 else -1
        accs.append(partial(which, lax.rem(me - sign + 2 * n, n)))
    for step in range(n - 1):
        sent = []
        for which in range(2):
            shift = shifts[which]
            perm = [(i, (i + shift) % n) for i in range(n)]
            sent.append(lax.ppermute(accs[which].astype(jnp.bfloat16), "head", perm))
        for which in range(2):
            sign = 1 if which == 0 else -1
            group = lax.rem(me - sign * (step + 2) + 4 * n, n)
            accs[which] = sent[which].astype(jnp.float32) + partial(which, group)
    return jnp.concatenate([accs[0], accs[1]], axis=0).astype(jnp.bfloat16)


def local(n_seq, cached_probs, out_old, key_lists, changed_block_numbers, delta_v, w_out):
    blocks_here = cached_probs.shape[0]
    heads_here = cached_probs.shape[1]
    topk_here = cached_probs.shape[2]
    values_here = heads_here // GROUP
    w_full = lax.all_gather(w_out, "seq", axis=1, tiled=True)
    every_change = gather_seq(delta_v, n_seq)
    every_change = every_change.reshape(n_seq * delta_v.shape[0] // BLK, BLK * values_here * HD)
    flat_lists = key_lists.reshape(blocks_here * topk_here)
    onehot = (flat_lists[:, None] == changed_block_numbers[None, :]).astype(jnp.bfloat16)
    selected = jnp.dot(onehot, every_change, preferred_element_type=jnp.float32)
    picked = selected.astype(jnp.bfloat16).reshape(blocks_here, topk_here, BLK, values_here, HD)
    tiles = cached_probs.reshape(blocks_here, values_here, GROUP, topk_here, BLK, BLK)
    delta_out = jnp.einsum("qvgkij,qkjvd->qivgd", tiles, picked, preferred_element_type=jnp.float32)
    delta_out = delta_out.reshape(blocks_here * BLK, heads_here * HD)
    attn_new = (out_old.astype(jnp.float32) + delta_out).astype(jnp.bfloat16)
    out_proj = ring_reduce_scatter(attn_new, w_full)
    return (attn_new, out_proj)


def solution(mesh):
    placed = (
        P("seq", "head", None, None, None),
        P("seq", "head"),
        P("seq", None),
        P(),
        P("seq", "head"),
        P("head", "seq"),
    )
    n_seq = mesh.shape["seq"]
    return jax.shard_map(
        lambda *a: local(n_seq, *a),
        mesh=mesh,
        in_specs=placed,
        out_specs=(P("seq", "head"), P("seq", "head")),
        check_vma=False,
    )
```

```python
import jax
import jax.numpy as jnp
from jax import lax
from jax.experimental import pallas as pl
from jax.experimental.pallas import tpu as pltpu
from jax.sharding import PartitionSpec as P

HD = 128
BLK = 128
GROUP = 5


def _gather_kernel(nx, nz, x_ref, o_ref, send1, recv1, send2, recv2, local_sem):
    me = lax.axis_index("seq")
    hh = lax.axis_index("head")
    mx = me // nz
    mz = lax.rem(me, nz)
    own = pltpu.make_async_copy(x_ref, o_ref.at[me], local_sem)
    own.start()
    first = []
    for k in range(1, nz):
        peer = mx * nz + lax.rem(mz + k, nz)
        copy = pltpu.make_async_remote_copy(
            src_ref=x_ref,
            dst_ref=o_ref.at[me],
            send_sem=send1.at[k],
            recv_sem=recv1.at[k],
            device_id=(peer, hh),
            device_id_type=pl.DeviceIdType.MESH,
        )
        copy.start()
        first.append(copy)
    own.wait()
    for copy in first:
        copy.wait_recv()
    row = pl.ds(pl.multiple_of(mx * nz, nz), nz)
    second = []
    for k in range(1, nx):
        peer = lax.rem(mx + k, nx) * nz + mz
        copy = pltpu.make_async_remote_copy(
            src_ref=o_ref.at[row],
            dst_ref=o_ref.at[row],
            send_sem=send2.at[k],
            recv_sem=recv2.at[k],
            device_id=(peer, hh),
            device_id_type=pl.DeviceIdType.MESH,
        )
        copy.start()
        second.append(copy)
    for copy in first:
        copy.wait_send()
    for copy in second:
        copy.wait_send()
    for copy in second:
        copy.wait_recv()


def gather_seq(x, nx, nz):
    n = nx * nz
    return pl.pallas_call(
        lambda *refs: _gather_kernel(nx, nz, *refs),
        out_shape=jax.ShapeDtypeStruct((n,) + x.shape, x.dtype),
        in_specs=[pl.BlockSpec(memory_space=pl.ANY)],
        out_specs=pl.BlockSpec(memory_space=pl.ANY),
        scratch_shapes=[
            pltpu.SemaphoreType.DMA((nz,)),
            pltpu.SemaphoreType.DMA((nz,)),
            pltpu.SemaphoreType.DMA((nx,)),
            pltpu.SemaphoreType.DMA((nx,)),
            pltpu.SemaphoreType.DMA,
        ],
        compiler_params=pltpu.CompilerParams(has_side_effects=True),
    )(x)


def local(nx, nz, cached_probs, out_old, key_lists, changed_block_numbers, delta_v, w_out):
    blocks_here = cached_probs.shape[0]
    heads_here = cached_probs.shape[1]
    topk_here = cached_probs.shape[2]
    values_here = heads_here // GROUP
    w_full = lax.all_gather(w_out, "seq", axis=1, tiled=True)
    every_change = gather_seq(delta_v, nx, nz)
    every_change = every_change.reshape(nx * nz * delta_v.shape[0] // BLK, BLK * values_here * HD)
    flat_lists = key_lists.reshape(blocks_here * topk_here)
    onehot = (flat_lists[:, None] == changed_block_numbers[None, :]).astype(jnp.bfloat16)
    selected = jnp.dot(onehot, every_change, preferred_element_type=jnp.float32)
    picked = selected.astype(jnp.bfloat16).reshape(blocks_here, topk_here, BLK, values_here, HD)
    tiles = cached_probs.reshape(blocks_here, values_here, GROUP, topk_here, BLK, BLK)
    delta_out = jnp.einsum("qvgkij,qkjvd->qivgd", tiles, picked, preferred_element_type=jnp.float32)
    delta_out = delta_out.reshape(blocks_here * BLK, heads_here * HD)
    attn_new = (out_old.astype(jnp.float32) + delta_out).astype(jnp.bfloat16)
    n_head = w_full.shape[1] // attn_new.shape[1]
    w_groups = w_full.reshape(w_full.shape[0], n_head, attn_new.shape[1])
    terms = jnp.einsum("tk,kgc->gtc", attn_new, w_groups, preferred_element_type=jnp.float32)
    out_proj = lax.psum_scatter(terms.astype(jnp.bfloat16), "head", scatter_dimension=0, tiled=True)[0]
    return (attn_new, out_proj)


def solution(mesh):
    placed = (
        P("seq", "head", None, None, None),
        P("seq", "head"),
        P("seq", None),
        P(),
        P("seq", "head"),
        P("head", "seq"),
    )
    n_seq = mesh.shape["seq"]
    nz = 8 if n_seq % 8 == 0 else n_seq
    return jax.shard_map(
        lambda *a: local(n_seq // nz, nz, *a),
        mesh=mesh,
        in_specs=placed,
        out_specs=(P("seq", "head"), P("seq", "head")),
        check_vma=False,
    )
```

```python
import jax
import jax.numpy as jnp
from jax import lax
from jax.experimental import pallas as pl
from jax.experimental.pallas import tpu as pltpu
from jax.sharding import PartitionSpec as P

HD = 128
BLK = 128
GROUP = 5


def _gather_kernel(nx, nz, x_ref, o_ref, send1, recv1, send2, recv2, local_sem):
    me = lax.axis_index("seq")
    hh = lax.axis_index("head")
    mx = me // nz
    mz = lax.rem(me, nz)
    own = pltpu.make_async_copy(x_ref, o_ref.at[me], local_sem)
    own.start()
    first = []
    for k in range(1, nz):
        peer = mx * nz + lax.rem(mz + k, nz)
        copy = pltpu.make_async_remote_copy(
            src_ref=x_ref,
            dst_ref=o_ref.at[me],
            send_sem=send1.at[k],
            recv_sem=recv1.at[k],
            device_id=(peer, hh),
            device_id_type=pl.DeviceIdType.MESH,
        )
        copy.start()
        first.append(copy)
    own.wait()
    for copy in first:
        copy.wait_recv()
    row = pl.ds(pl.multiple_of(mx * nz, nz), nz)
    second = []
    for k in range(1, nx):
        peer = lax.rem(mx + k, nx) * nz + mz
        copy = pltpu.make_async_remote_copy(
            src_ref=o_ref.at[row],
            dst_ref=o_ref.at[row],
            send_sem=send2.at[k],
            recv_sem=recv2.at[k],
            device_id=(peer, hh),
            device_id_type=pl.DeviceIdType.MESH,
        )
        copy.start()
        second.append(copy)
    for copy in first:
        copy.wait_send()
    for copy in second:
        copy.wait_send()
    for copy in second:
        copy.wait_recv()


def gather_seq(x, nx, nz):
    n = nx * nz
    return pl.pallas_call(
        lambda *refs: _gather_kernel(nx, nz, *refs),
        out_shape=jax.ShapeDtypeStruct((n,) + x.shape, x.dtype),
        in_specs=[pl.BlockSpec(memory_space=pl.ANY)],
        out_specs=pl.BlockSpec(memory_space=pl.ANY),
        scratch_shapes=[
            pltpu.SemaphoreType.DMA((nz,)),
            pltpu.SemaphoreType.DMA((nz,)),
            pltpu.SemaphoreType.DMA((nx,)),
            pltpu.SemaphoreType.DMA((nx,)),
            pltpu.SemaphoreType.DMA,
        ],
        compiler_params=pltpu.CompilerParams(has_side_effects=True),
    )(x)


def _project_kernel(a_ref, w_ref, o_ref):
    term = lax.dot_general(a_ref[...], w_ref[...], (((1,), (1,)), ((), ())), preferred_element_type=jnp.float32)
    o_ref[0] = term.astype(o_ref.dtype)


def project(a, w_t):
    rows, width = a.shape
    groups = w_t.shape[0] // width
    return pl.pallas_call(
        _project_kernel,
        out_shape=jax.ShapeDtypeStruct((groups, rows, width), a.dtype),
        grid=(groups,),
        in_specs=[
            pl.BlockSpec((rows, width), lambda g: (0, 0)),
            pl.BlockSpec((width, w_t.shape[1]), lambda g: (g, 0)),
        ],
        out_specs=pl.BlockSpec((1, rows, width), lambda g: (g, 0, 0)),
        cost_estimate=pl.CostEstimate(
            flops=2 * rows * width * w_t.shape[0],
            bytes_accessed=2 * (a.size + w_t.size + groups * rows * width),
            transcendentals=0,
        ),
    )(a, w_t)


def local(nx, nz, cached_probs, out_old, key_lists, changed_block_numbers, delta_v, w_out):
    blocks_here = cached_probs.shape[0]
    heads_here = cached_probs.shape[1]
    topk_here = cached_probs.shape[2]
    values_here = heads_here // GROUP
    w_full = lax.all_gather(w_out, "seq", axis=1, tiled=True)
    every_change = gather_seq(delta_v, nx, nz)
    every_change = every_change.reshape(nx * nz * delta_v.shape[0] // BLK, BLK * values_here * HD)
    flat_lists = key_lists.reshape(blocks_here * topk_here)
    onehot = (flat_lists[:, None] == changed_block_numbers[None, :]).astype(jnp.bfloat16)
    selected = jnp.dot(onehot, every_change, preferred_element_type=jnp.float32)
    picked = selected.astype(jnp.bfloat16).reshape(blocks_here, topk_here, BLK, values_here, HD)
    tiles = cached_probs.reshape(blocks_here, values_here, GROUP, topk_here, BLK, BLK)
    delta_out = jnp.einsum("qvgkij,qkjvd->qivgd", tiles, picked, preferred_element_type=jnp.float32)
    delta_out = delta_out.reshape(blocks_here * BLK, heads_here * HD)
    attn_new = (out_old.astype(jnp.float32) + delta_out).astype(jnp.bfloat16)
    terms = project(attn_new, w_full.T)
    out_proj = lax.psum_scatter(terms.astype(jnp.bfloat16), "head", scatter_dimension=0, tiled=True)[0]
    return (attn_new, out_proj)


def solution(mesh):
    placed = (
        P("seq", "head", None, None, None),
        P("seq", "head"),
        P("seq", None),
        P(),
        P("seq", "head"),
        P("head", "seq"),
    )
    n_seq = mesh.shape["seq"]
    nz = 8 if n_seq % 8 == 0 else n_seq
    return jax.shard_map(
        lambda *a: local(n_seq // nz, nz, *a),
        mesh=mesh,
        in_specs=placed,
        out_specs=(P("seq", "head"), P("seq", "head")),
        check_vma=False,
    )
```

```python
import jax
import jax.numpy as jnp
from jax import lax
from jax.experimental import pallas as pl
from jax.experimental.pallas import tpu as pltpu
from jax.sharding import PartitionSpec as P

HD = 128
BLK = 128
GROUP = 5


def _gather_kernel(nx, nz, x_ref, o_ref, send1, recv1, send2, recv2, local_sem):
    me = lax.axis_index("seq")
    hh = lax.axis_index("head")
    mx = me // nz
    mz = lax.rem(me, nz)
    own = pltpu.make_async_copy(x_ref, o_ref.at[me], local_sem)
    own.start()
    first = []
    for k in range(1, nz):
        peer = mx * nz + lax.rem(mz + k, nz)
        copy = pltpu.make_async_remote_copy(
            src_ref=x_ref,
            dst_ref=o_ref.at[me],
            send_sem=send1.at[k],
            recv_sem=recv1.at[k],
            device_id=(peer, hh),
            device_id_type=pl.DeviceIdType.MESH,
        )
        copy.start()
        first.append(copy)
    own.wait()
    for copy in first:
        copy.wait_recv()
    row = pl.ds(pl.multiple_of(mx * nz, nz), nz)
    second = []
    for k in range(1, nx):
        peer = lax.rem(mx + k, nx) * nz + mz
        copy = pltpu.make_async_remote_copy(
            src_ref=o_ref.at[row],
            dst_ref=o_ref.at[row],
            send_sem=send2.at[k],
            recv_sem=recv2.at[k],
            device_id=(peer, hh),
            device_id_type=pl.DeviceIdType.MESH,
        )
        copy.start()
        second.append(copy)
    for copy in first:
        copy.wait_send()
    for copy in second:
        copy.wait_send()
    for copy in second:
        copy.wait_recv()


def gather_seq(x, nx, nz):
    n = nx * nz
    return pl.pallas_call(
        lambda *refs: _gather_kernel(nx, nz, *refs),
        out_shape=jax.ShapeDtypeStruct((n,) + x.shape, x.dtype),
        in_specs=[pl.BlockSpec(memory_space=pl.ANY)],
        out_specs=pl.BlockSpec(memory_space=pl.ANY),
        scratch_shapes=[
            pltpu.SemaphoreType.DMA((nz,)),
            pltpu.SemaphoreType.DMA((nz,)),
            pltpu.SemaphoreType.DMA((nx,)),
            pltpu.SemaphoreType.DMA((nx,)),
            pltpu.SemaphoreType.DMA,
        ],
        compiler_params=pltpu.CompilerParams(has_side_effects=True),
    )(x)


def local(nx, nz, cached_probs, out_old, key_lists, changed_block_numbers, delta_v, w_out):
    blocks_here = cached_probs.shape[0]
    heads_here = cached_probs.shape[1]
    topk_here = cached_probs.shape[2]
    values_here = heads_here // GROUP
    w_full = lax.all_gather(w_out, "seq", axis=1, tiled=True)
    every_change = gather_seq(delta_v, nx, nz)
    every_change, cached_probs = lax.optimization_barrier((every_change, cached_probs))
    every_change = every_change.reshape(nx * nz * delta_v.shape[0] // BLK, BLK * values_here * HD)
    flat_lists = key_lists.reshape(blocks_here * topk_here)
    onehot = (flat_lists[:, None] == changed_block_numbers[None, :]).astype(jnp.bfloat16)
    selected = jnp.dot(onehot, every_change, preferred_element_type=jnp.float32)
    picked = selected.astype(jnp.bfloat16).reshape(blocks_here, topk_here, BLK, values_here, HD)
    tiles = cached_probs.reshape(blocks_here, values_here, GROUP, topk_here, BLK, BLK)
    delta_out = jnp.einsum("qvgkij,qkjvd->qivgd", tiles, picked, preferred_element_type=jnp.float32)
    delta_out = delta_out.reshape(blocks_here * BLK, heads_here * HD)
    attn_new = (out_old.astype(jnp.float32) + delta_out).astype(jnp.bfloat16)
    n_head = w_full.shape[1] // attn_new.shape[1]
    w_groups = w_full.reshape(w_full.shape[0], n_head, attn_new.shape[1])
    terms = jnp.einsum("tk,kgc->gtc", attn_new, w_groups, preferred_element_type=jnp.float32)
    out_proj = lax.psum_scatter(terms.astype(jnp.bfloat16), "head", scatter_dimension=0, tiled=True)[0]
    return (attn_new, out_proj)


def solution(mesh):
    placed = (
        P("seq", "head", None, None, None),
        P("seq", "head"),
        P("seq", None),
        P(),
        P("seq", "head"),
        P("head", "seq"),
    )
    n_seq = mesh.shape["seq"]
    nz = 8 if n_seq % 8 == 0 else n_seq
    return jax.shard_map(
        lambda *a: local(n_seq // nz, nz, *a),
        mesh=mesh,
        in_specs=placed,
        out_specs=(P("seq", "head"), P("seq", "head")),
        check_vma=False,
    )
```

```python
import jax
import jax.numpy as jnp
from jax import lax
from jax.experimental import pallas as pl
from jax.experimental.pallas import tpu as pltpu
from jax.sharding import Mesh, PartitionSpec as P

HD = 128
BLK = 128
GROUP = 5


def _gather_kernel(nx, nz, x_ref, o_ref, send1, recv1, send2, recv2, local_sem):
    mx = lax.axis_index("sx")
    mz = lax.axis_index("sz")
    hh = lax.axis_index("head")
    me = mx * nz + mz
    own = pltpu.make_async_copy(x_ref, o_ref.at[me], local_sem)
    own.start()
    first = []
    for k in range(1, nz):
        peer = lax.rem(mz + k, nz)
        copy = pltpu.make_async_remote_copy(
            src_ref=x_ref,
            dst_ref=o_ref.at[me],
            send_sem=send1.at[k],
            recv_sem=recv1.at[k],
            device_id=(mx, peer, hh),
            device_id_type=pl.DeviceIdType.MESH,
        )
        copy.start()
        first.append(copy)
    own.wait()
    for copy in first:
        copy.wait_recv()
    row = pl.ds(pl.multiple_of(mx * nz, nz), nz)
    second = []
    for k in range(1, nx):
        peer = lax.rem(mx + k, nx)
        copy = pltpu.make_async_remote_copy(
            src_ref=o_ref.at[row],
            dst_ref=o_ref.at[row],
            send_sem=send2.at[k],
            recv_sem=recv2.at[k],
            device_id=(peer, mz, hh),
            device_id_type=pl.DeviceIdType.MESH,
        )
        copy.start()
        second.append(copy)
    for copy in first:
        copy.wait_send()
    for copy in second:
        copy.wait_send()
    for copy in second:
        copy.wait_recv()


def _gather_x_kernel(nx, x_ref, o_ref, send_sem, recv_sem, local_sem):
    mx = lax.axis_index("sx")
    mz = lax.axis_index("sz")
    hh = lax.axis_index("head")
    own = pltpu.make_async_copy(x_ref, o_ref.at[mx], local_sem)
    own.start()
    copies = []
    for k in range(1, nx):
        copy = pltpu.make_async_remote_copy(
            src_ref=x_ref,
            dst_ref=o_ref.at[mx],
            send_sem=send_sem.at[k],
            recv_sem=recv_sem.at[k],
            device_id=(lax.rem(mx + k, nx), mz, hh),
            device_id_type=pl.DeviceIdType.MESH,
        )
        copy.start()
        copies.append(copy)
    for copy in copies:
        copy.wait_send()
    for copy in copies:
        copy.wait_recv()
    own.wait()


def gather_x(x, nx):
    return pl.pallas_call(
        lambda *refs: _gather_x_kernel(nx, *refs),
        out_shape=jax.ShapeDtypeStruct((nx,) + x.shape, x.dtype),
        in_specs=[pl.BlockSpec(memory_space=pl.ANY)],
        out_specs=pl.BlockSpec(memory_space=pl.ANY),
        scratch_shapes=[
            pltpu.SemaphoreType.DMA((nx,)),
            pltpu.SemaphoreType.DMA((nx,)),
            pltpu.SemaphoreType.DMA,
        ],
        compiler_params=pltpu.CompilerParams(has_side_effects=True),
    )(x)


def gather_seq(x, nx, nz):
    n = nx * nz
    return pl.pallas_call(
        lambda *refs: _gather_kernel(nx, nz, *refs),
        out_shape=jax.ShapeDtypeStruct((n,) + x.shape, x.dtype),
        in_specs=[pl.BlockSpec(memory_space=pl.ANY)],
        out_specs=pl.BlockSpec(memory_space=pl.ANY),
        scratch_shapes=[
            pltpu.SemaphoreType.DMA((nz,)),
            pltpu.SemaphoreType.DMA((nz,)),
            pltpu.SemaphoreType.DMA((nx,)),
            pltpu.SemaphoreType.DMA((nx,)),
            pltpu.SemaphoreType.DMA,
        ],
        compiler_params=pltpu.CompilerParams(has_side_effects=True),
    )(x)


def local(nx, nz, cached_probs, out_old, key_lists, changed_block_numbers, delta_v, w_out):
    blocks_here = cached_probs.shape[0]
    heads_here = cached_probs.shape[1]
    topk_here = cached_probs.shape[2]
    values_here = heads_here // GROUP
    w_rows = lax.all_gather(gather_x(w_out, nx), "sz", axis=0, tiled=False)
    every_change = gather_seq(delta_v, nx, nz)
    every_change, cached_probs = lax.optimization_barrier((every_change, cached_probs))
    every_change = every_change.reshape(nx * nz * delta_v.shape[0] // BLK, BLK * values_here * HD)
    flat_lists = key_lists.reshape(blocks_here * topk_here)
    onehot = (flat_lists[:, None] == changed_block_numbers[None, :]).astype(jnp.bfloat16)
    selected = jnp.dot(onehot, every_change, preferred_element_type=jnp.float32)
    picked = selected.astype(jnp.bfloat16).reshape(blocks_here, topk_here, BLK, values_here, HD)
    tiles = cached_probs.reshape(blocks_here, values_here, GROUP, topk_here, BLK, BLK)
    delta_out = jnp.einsum("qvgkij,qkjvd->qivgd", tiles, picked, preferred_element_type=jnp.float32)
    delta_out = delta_out.reshape(blocks_here * BLK, heads_here * HD)
    attn_new = (out_old.astype(jnp.float32) + delta_out).astype(jnp.bfloat16)
    width = attn_new.shape[1]
    per_group = width // w_out.shape[1]
    halves = nz // per_group
    w_split = w_rows.reshape(halves, per_group, nx, w_out.shape[0], w_out.shape[1])
    terms = jnp.einsum("tk,hlxkc->xhtlc", attn_new, w_split, preferred_element_type=jnp.float32)
    terms = terms.reshape(nx * halves, attn_new.shape[0], width)
    out_proj = lax.psum_scatter(terms.astype(jnp.bfloat16), "head", scatter_dimension=0, tiled=True)[0]
    return (attn_new, out_proj)


def solution(mesh):
    n_seq = mesh.shape["seq"]
    nz = 8 if n_seq % 8 == 0 else n_seq
    nx = n_seq // nz
    split = Mesh(mesh.devices.reshape(nx, nz, mesh.shape["head"]), ("sx", "sz", "head"))
    seq = ("sx", "sz")
    placed = (
        P(seq, "head", None, None, None),
        P(seq, "head"),
        P(seq, None),
        P(),
        P(seq, "head"),
        P("head", seq),
    )
    return jax.shard_map(
        lambda *a: local(nx, nz, *a),
        mesh=split,
        in_specs=placed,
        out_specs=(P(seq, "head"), P(seq, "head")),
        check_vma=False,
    )
```

```python
import jax
import jax.numpy as jnp
from jax import lax
from jax.experimental import pallas as pl
from jax.experimental.pallas import tpu as pltpu
from jax.sharding import Mesh, PartitionSpec as P

HD = 128
BLK = 128
GROUP = 5


def _gather_kernel(nx, nz, x_ref, o_ref, send1, recv1, send2, recv2, local_sem):
    me = lax.axis_index("seq")
    hy = lax.axis_index("hy")
    hc = lax.axis_index("hc")
    mx = me // nz
    mz = lax.rem(me, nz)
    own = pltpu.make_async_copy(x_ref, o_ref.at[me], local_sem)
    own.start()
    first = []
    for k in range(1, nz):
        peer = mx * nz + lax.rem(mz + k, nz)
        copy = pltpu.make_async_remote_copy(
            src_ref=x_ref,
            dst_ref=o_ref.at[me],
            send_sem=send1.at[k],
            recv_sem=recv1.at[k],
            device_id=(peer, hy, hc),
            device_id_type=pl.DeviceIdType.MESH,
        )
        copy.start()
        first.append(copy)
    own.wait()
    for copy in first:
        copy.wait_recv()
    row = pl.ds(pl.multiple_of(mx * nz, nz), nz)
    second = []
    for k in range(1, nx):
        peer = lax.rem(mx + k, nx) * nz + mz
        copy = pltpu.make_async_remote_copy(
            src_ref=o_ref.at[row],
            dst_ref=o_ref.at[row],
            send_sem=send2.at[k],
            recv_sem=recv2.at[k],
            device_id=(peer, hy, hc),
            device_id_type=pl.DeviceIdType.MESH,
        )
        copy.start()
        second.append(copy)
    for copy in first:
        copy.wait_send()
    for copy in second:
        copy.wait_send()
    for copy in second:
        copy.wait_recv()


def gather_seq(x, nx, nz):
    n = nx * nz
    return pl.pallas_call(
        lambda *refs: _gather_kernel(nx, nz, *refs),
        out_shape=jax.ShapeDtypeStruct((n,) + x.shape, x.dtype),
        in_specs=[pl.BlockSpec(memory_space=pl.ANY)],
        out_specs=pl.BlockSpec(memory_space=pl.ANY),
        scratch_shapes=[
            pltpu.SemaphoreType.DMA((nz,)),
            pltpu.SemaphoreType.DMA((nz,)),
            pltpu.SemaphoreType.DMA((nx,)),
            pltpu.SemaphoreType.DMA((nx,)),
            pltpu.SemaphoreType.DMA,
        ],
        compiler_params=pltpu.CompilerParams(has_side_effects=True),
    )(x)


def local(nx, nz, cached_probs, out_old, key_lists, changed_block_numbers, delta_v, w_out):
    blocks_here = cached_probs.shape[0]
    heads_here = cached_probs.shape[1]
    topk_here = cached_probs.shape[2]
    values_here = heads_here // GROUP
    w_full = lax.all_gather(w_out, "seq", axis=1, tiled=True)
    every_change = gather_seq(delta_v, nx, nz)
    every_change, cached_probs = lax.optimization_barrier((every_change, cached_probs))
    every_change = every_change.reshape(nx * nz * delta_v.shape[0] // BLK, BLK * values_here * HD)
    flat_lists = key_lists.reshape(blocks_here * topk_here)
    onehot = (flat_lists[:, None] == changed_block_numbers[None, :]).astype(jnp.bfloat16)
    selected = jnp.dot(onehot, every_change, preferred_element_type=jnp.float32)
    picked = selected.astype(jnp.bfloat16).reshape(blocks_here, topk_here, BLK, values_here, HD)
    tiles = cached_probs.reshape(blocks_here, values_here, GROUP, topk_here, BLK, BLK)
    delta_out = jnp.einsum("qvgkij,qkjvd->qivgd", tiles, picked, preferred_element_type=jnp.float32)
    delta_out = delta_out.reshape(blocks_here * BLK, heads_here * HD)
    attn_new = (out_old.astype(jnp.float32) + delta_out).astype(jnp.bfloat16)
    n_head = w_full.shape[1] // attn_new.shape[1]
    width = attn_new.shape[1]
    w_pairs = w_full.reshape(w_full.shape[0], n_head // 2, 2, width)
    core = lax.axis_index("hc")
    theirs = jnp.einsum("tk,kpc->ptc", attn_new, lax.dynamic_index_in_dim(w_pairs, 1 - core, axis=2, keepdims=False),
                        preferred_element_type=jnp.float32).astype(jnp.bfloat16)
    arrived = lax.ppermute(theirs, "hc", [(0, 1), (1, 0)])
    mine = jnp.einsum("tk,kpc->ptc", attn_new, lax.dynamic_index_in_dim(w_pairs, core, axis=2, keepdims=False),
                      preferred_element_type=jnp.float32).astype(jnp.bfloat16)
    mine = lax.optimization_barrier(mine)
    pair_sum = (mine.astype(jnp.float32) + arrived.astype(jnp.float32)).astype(jnp.bfloat16)
    out_proj = lax.psum_scatter(pair_sum, "hy", scatter_dimension=0, tiled=True)[0]
    return (attn_new, out_proj)


def solution(mesh):
    head = ("hy", "hc")
    placed = (
        P("seq", head, None, None, None),
        P("seq", head),
        P("seq", None),
        P(),
        P("seq", head),
        P(head, "seq"),
    )
    n_seq = mesh.shape["seq"]
    nz = 8 if n_seq % 8 == 0 else n_seq
    split = Mesh(mesh.devices.reshape(n_seq, mesh.shape["head"] // 2, 2), ("seq", "hy", "hc"))
    return jax.shard_map(
        lambda *a: local(n_seq // nz, nz, *a),
        mesh=split,
        in_specs=placed,
        out_specs=(P("seq", head), P("seq", head)),
        check_vma=False,
    )
```

```python
import jax
import jax.numpy as jnp
from jax import lax
from jax.experimental import pallas as pl
from jax.experimental.pallas import tpu as pltpu
from jax.sharding import Mesh, PartitionSpec as P

HD = 128
BLK = 128
GROUP = 5


def _gather_kernel(nx, nz, x_ref, o_ref, send1, recv1, send2, recv2, local_sem):
    me = lax.axis_index("seq")
    hy = lax.axis_index("hy")
    hc = lax.axis_index("hc")
    mx = me // nz
    mz = lax.rem(me, nz)
    own = pltpu.make_async_copy(x_ref, o_ref.at[me], local_sem)
    own.start()
    first = []
    for k in range(1, nz):
        peer = mx * nz + lax.rem(mz + k, nz)
        copy = pltpu.make_async_remote_copy(
            src_ref=x_ref,
            dst_ref=o_ref.at[me],
            send_sem=send1.at[k],
            recv_sem=recv1.at[k],
            device_id=(peer, hy, hc),
            device_id_type=pl.DeviceIdType.MESH,
        )
        copy.start()
        first.append(copy)
    own.wait()
    for copy in first:
        copy.wait_recv()
    row = pl.ds(pl.multiple_of(mx * nz, nz), nz)
    second = []
    for k in range(1, nx):
        peer = lax.rem(mx + k, nx) * nz + mz
        copy = pltpu.make_async_remote_copy(
            src_ref=o_ref.at[row],
            dst_ref=o_ref.at[row],
            send_sem=send2.at[k],
            recv_sem=recv2.at[k],
            device_id=(peer, hy, hc),
            device_id_type=pl.DeviceIdType.MESH,
        )
        copy.start()
        second.append(copy)
    for copy in first:
        copy.wait_send()
    for copy in second:
        copy.wait_send()
    for copy in second:
        copy.wait_recv()


def gather_seq(x, nx, nz):
    n = nx * nz
    return pl.pallas_call(
        lambda *refs: _gather_kernel(nx, nz, *refs),
        out_shape=jax.ShapeDtypeStruct((n,) + x.shape, x.dtype),
        in_specs=[pl.BlockSpec(memory_space=pl.ANY)],
        out_specs=pl.BlockSpec(memory_space=pl.ANY),
        scratch_shapes=[
            pltpu.SemaphoreType.DMA((nz,)),
            pltpu.SemaphoreType.DMA((nz,)),
            pltpu.SemaphoreType.DMA((nx,)),
            pltpu.SemaphoreType.DMA((nx,)),
            pltpu.SemaphoreType.DMA,
        ],
        compiler_params=pltpu.CompilerParams(has_side_effects=True),
    )(x)


def local(nx, nz, cached_probs, out_old, key_lists, changed_block_numbers, delta_v, w_out):
    blocks_here = cached_probs.shape[0]
    heads_here = cached_probs.shape[1]
    topk_here = cached_probs.shape[2]
    values_here = heads_here // GROUP
    w_full = lax.all_gather(w_out, "seq", axis=1, tiled=True)
    every_change = gather_seq(delta_v, nx, nz)
    every_change, cached_probs = lax.optimization_barrier((every_change, cached_probs))
    every_change = every_change.reshape(nx * nz * delta_v.shape[0] // BLK, BLK * values_here * HD)
    flat_lists = key_lists.reshape(blocks_here * topk_here)
    onehot = (flat_lists[:, None] == changed_block_numbers[None, :]).astype(jnp.bfloat16)
    selected = jnp.dot(onehot, every_change, preferred_element_type=jnp.float32)
    picked = selected.astype(jnp.bfloat16).reshape(blocks_here, topk_here, BLK, values_here, HD)
    tiles = cached_probs.reshape(blocks_here, values_here, GROUP, topk_here, BLK, BLK)
    delta_out = jnp.einsum("qvgkij,qkjvd->qivgd", tiles, picked, preferred_element_type=jnp.float32)
    delta_out = delta_out.reshape(blocks_here * BLK, heads_here * HD)
    attn_new = (out_old.astype(jnp.float32) + delta_out).astype(jnp.bfloat16)
    n_head = w_full.shape[1] // attn_new.shape[1]
    width = attn_new.shape[1]
    w_pairs = w_full.reshape(w_full.shape[0], n_head // 2, 2, width)
    core = lax.axis_index("hc")
    theirs_w = lax.dynamic_index_in_dim(w_pairs, 1 - core, axis=2, keepdims=False)
    mine_w = lax.dynamic_index_in_dim(w_pairs, core, axis=2, keepdims=False)
    chunk = n_head // 4
    sums = []
    arrivals = []
    for part in range(2):
        cols = theirs_w[:, part * chunk:(part + 1) * chunk]
        theirs = jnp.einsum("tk,kpc->ptc", attn_new, cols, preferred_element_type=jnp.float32).astype(jnp.bfloat16)
        arrivals.append(lax.ppermute(theirs, "hc", [(0, 1), (1, 0)]))
    for part in range(2):
        cols = mine_w[:, part * chunk:(part + 1) * chunk]
        mine = jnp.einsum("tk,kpc->ptc", attn_new, cols, preferred_element_type=jnp.float32).astype(jnp.bfloat16)
        sums.append((mine.astype(jnp.float32) + arrivals[part].astype(jnp.float32)).astype(jnp.bfloat16))
    pair_sum = jnp.concatenate(sums, axis=0)
    out_proj = lax.psum_scatter(pair_sum, "hy", scatter_dimension=0, tiled=True)[0]
    return (attn_new, out_proj)


def solution(mesh):
    head = ("hy", "hc")
    placed = (
        P("seq", head, None, None, None),
        P("seq", head),
        P("seq", None),
        P(),
        P("seq", head),
        P(head, "seq"),
    )
    n_seq = mesh.shape["seq"]
    nz = 8 if n_seq % 8 == 0 else n_seq
    split = Mesh(mesh.devices.reshape(n_seq, mesh.shape["head"] // 2, 2), ("seq", "hy", "hc"))
    return jax.shard_map(
        lambda *a: local(n_seq // nz, nz, *a),
        mesh=split,
        in_specs=placed,
        out_specs=(P("seq", head), P("seq", head)),
        check_vma=False,
    )
```

```python
import jax
import jax.numpy as jnp
from jax import lax
from jax.experimental import pallas as pl
from jax.experimental.pallas import tpu as pltpu
from jax.sharding import PartitionSpec as P

HD = 128
BLK = 128
GROUP = 5


def _gather_kernel(nx, nz, x_ref, o_ref, send1, recv1, send2, recv2, local_sem):
    me = lax.axis_index("seq")
    hh = lax.axis_index("head")
    mx = me // nz
    mz = lax.rem(me, nz)
    own = pltpu.make_async_copy(x_ref, o_ref.at[me], local_sem)
    own.start()
    first = []
    for k in range(1, nz):
        peer = mx * nz + lax.rem(mz + k, nz)
        copy = pltpu.make_async_remote_copy(
            src_ref=x_ref,
            dst_ref=o_ref.at[me],
            send_sem=send1.at[k],
            recv_sem=recv1.at[k],
            device_id=(peer, hh),
            device_id_type=pl.DeviceIdType.MESH,
        )
        copy.start()
        first.append(copy)
    own.wait()
    for copy in first:
        copy.wait_recv()
    row = pl.ds(pl.multiple_of(mx * nz, nz), nz)
    second = []
    for k in range(1, nx):
        peer = lax.rem(mx + k, nx) * nz + mz
        copy = pltpu.make_async_remote_copy(
            src_ref=o_ref.at[row],
            dst_ref=o_ref.at[row],
            send_sem=send2.at[k],
            recv_sem=recv2.at[k],
            device_id=(peer, hh),
            device_id_type=pl.DeviceIdType.MESH,
        )
        copy.start()
        second.append(copy)
    for copy in first:
        copy.wait_send()
    for copy in second:
        copy.wait_send()
    for copy in second:
        copy.wait_recv()


def gather_seq(x, nx, nz):
    n = nx * nz
    return pl.pallas_call(
        lambda *refs: _gather_kernel(nx, nz, *refs),
        out_shape=jax.ShapeDtypeStruct((n,) + x.shape, x.dtype),
        in_specs=[pl.BlockSpec(memory_space=pl.ANY)],
        out_specs=pl.BlockSpec(memory_space=pl.ANY),
        scratch_shapes=[
            pltpu.SemaphoreType.DMA((nz,)),
            pltpu.SemaphoreType.DMA((nz,)),
            pltpu.SemaphoreType.DMA((nx,)),
            pltpu.SemaphoreType.DMA((nx,)),
            pltpu.SemaphoreType.DMA,
        ],
        compiler_params=pltpu.CompilerParams(has_side_effects=True),
    )(x)


def _project_kernel(w_ref, a_ref, o_ref):
    o_ref[0] = jnp.dot(w_ref[...], a_ref[...], preferred_element_type=jnp.float32).astype(o_ref.dtype)


def project_t(w_t, a_t):
    width, rows = a_t.shape
    groups = w_t.shape[0] // width
    return pl.pallas_call(
        _project_kernel,
        out_shape=jax.ShapeDtypeStruct((groups, width, rows), a_t.dtype),
        grid=(groups,),
        in_specs=[
            pl.BlockSpec((width, w_t.shape[1]), lambda g: (g, 0)),
            pl.BlockSpec((width, rows), lambda g: (0, 0)),
        ],
        out_specs=pl.BlockSpec((1, width, rows), lambda g: (g, 0, 0)),
        cost_estimate=pl.CostEstimate(
            flops=2 * rows * width * w_t.shape[0],
            bytes_accessed=2 * (a_t.size + w_t.size + groups * rows * width),
            transcendentals=0,
        ),
    )(w_t, a_t)


def local(nx, nz, cached_probs, out_old, key_lists, changed_block_numbers, delta_v, w_out):
    blocks_here = cached_probs.shape[0]
    heads_here = cached_probs.shape[1]
    topk_here = cached_probs.shape[2]
    values_here = heads_here // GROUP
    w_full = lax.all_gather(w_out, "seq", axis=1, tiled=True)
    every_change = gather_seq(delta_v, nx, nz)
    every_change, cached_probs = lax.optimization_barrier((every_change, cached_probs))
    every_change = every_change.reshape(nx * nz * delta_v.shape[0] // BLK, BLK * values_here * HD)
    flat_lists = key_lists.reshape(blocks_here * topk_here)
    onehot = (flat_lists[:, None] == changed_block_numbers[None, :]).astype(jnp.bfloat16)
    selected = jnp.dot(onehot, every_change, preferred_element_type=jnp.float32)
    picked = selected.astype(jnp.bfloat16).reshape(blocks_here, topk_here, BLK, values_here, HD)
    tiles = cached_probs.reshape(blocks_here, values_here, GROUP, topk_here, BLK, BLK)
    delta_out = jnp.einsum("qvgkij,qkjvd->qivgd", tiles, picked, preferred_element_type=jnp.float32)
    delta_out = delta_out.reshape(blocks_here * BLK, heads_here * HD)
    attn_new = (out_old.astype(jnp.float32) + delta_out).astype(jnp.bfloat16)
    terms_t = project_t(w_full.T, attn_new.T)
    out_proj = lax.psum_scatter(terms_t, "head", scatter_dimension=0, tiled=True)[0].T
    return (attn_new, out_proj)


def solution(mesh):
    placed = (
        P("seq", "head", None, None, None),
        P("seq", "head"),
        P("seq", None),
        P(),
        P("seq", "head"),
        P("head", "seq"),
    )
    n_seq = mesh.shape["seq"]
    nz = 8 if n_seq % 8 == 0 else n_seq
    return jax.shard_map(
        lambda *a: local(n_seq // nz, nz, *a),
        mesh=mesh,
        in_specs=placed,
        out_specs=(P("seq", "head"), P("seq", "head")),
        check_vma=False,
    )
```

```python
import jax
import jax.numpy as jnp
from jax import lax
from jax.experimental import pallas as pl
from jax.experimental.pallas import tpu as pltpu
from jax.sharding import PartitionSpec as P

HD = 128
BLK = 128
GROUP = 5


def _gather_kernel(nx, nz, x_ref, o_ref, send1, recv1, send2, recv2, local_sem):
    me = lax.axis_index("seq")
    hh = lax.axis_index("head")
    mx = me // nz
    mz = lax.rem(me, nz)
    own = pltpu.make_async_copy(x_ref, o_ref.at[me], local_sem)
    own.start()
    first = []
    for k in range(1, nz):
        peer = mx * nz + lax.rem(mz + k, nz)
        copy = pltpu.make_async_remote_copy(
            src_ref=x_ref,
            dst_ref=o_ref.at[me],
            send_sem=send1.at[k],
            recv_sem=recv1.at[k],
            device_id=(peer, hh),
            device_id_type=pl.DeviceIdType.MESH,
        )
        copy.start()
        first.append(copy)
    own.wait()
    for copy in first:
        copy.wait_recv()
    row = pl.ds(pl.multiple_of(mx * nz, nz), nz)
    second = []
    for k in range(1, nx):
        peer = lax.rem(mx + k, nx) * nz + mz
        copy = pltpu.make_async_remote_copy(
            src_ref=o_ref.at[row],
            dst_ref=o_ref.at[row],
            send_sem=send2.at[k],
            recv_sem=recv2.at[k],
            device_id=(peer, hh),
            device_id_type=pl.DeviceIdType.MESH,
        )
        copy.start()
        second.append(copy)
    for copy in first:
        copy.wait_send()
    for copy in second:
        copy.wait_send()
    for copy in second:
        copy.wait_recv()


def gather_seq(x, nx, nz):
    n = nx * nz
    return pl.pallas_call(
        lambda *refs: _gather_kernel(nx, nz, *refs),
        out_shape=jax.ShapeDtypeStruct((n,) + x.shape, x.dtype),
        in_specs=[pl.BlockSpec(memory_space=pl.ANY)],
        out_specs=pl.BlockSpec(memory_space=pl.ANY),
        scratch_shapes=[
            pltpu.SemaphoreType.DMA((nz,)),
            pltpu.SemaphoreType.DMA((nz,)),
            pltpu.SemaphoreType.DMA((nx,)),
            pltpu.SemaphoreType.DMA((nx,)),
            pltpu.SemaphoreType.DMA,
        ],
        compiler_params=pltpu.CompilerParams(has_side_effects=True),
    )(x)


def _refresh_kernel(p_ref, v_ref, o_ref, out_ref):
    acc = o_ref[...].astype(jnp.float32)
    for k in range(p_ref.shape[2]):
        acc += jnp.dot(p_ref[0, 0, k], v_ref[0, k], preferred_element_type=jnp.float32)
    out_ref[...] = acc.astype(out_ref.dtype)


def refresh(cached_probs, picked, out_old):
    blocks, heads, topk = cached_probs.shape[:3]
    return pl.pallas_call(
        _refresh_kernel,
        out_shape=jax.ShapeDtypeStruct(out_old.shape, out_old.dtype),
        grid=(blocks, heads),
        in_specs=[
            pl.BlockSpec((1, 1, topk, BLK, BLK), lambda q, h: (q, h, 0, 0, 0)),
            pl.BlockSpec((1, topk, BLK, HD), lambda q, h: (q, 0, 0, h // GROUP)),
            pl.BlockSpec((BLK, HD), lambda q, h: (q, h)),
        ],
        out_specs=pl.BlockSpec((BLK, HD), lambda q, h: (q, h)),
        cost_estimate=pl.CostEstimate(
            flops=2 * blocks * heads * topk * BLK * BLK * HD,
            bytes_accessed=2 * (cached_probs.size + picked.size + 2 * out_old.size),
            transcendentals=0,
        ),
    )(cached_probs, picked, out_old)


def local(nx, nz, cached_probs, out_old, key_lists, changed_block_numbers, delta_v, w_out):
    blocks_here = cached_probs.shape[0]
    heads_here = cached_probs.shape[1]
    topk_here = cached_probs.shape[2]
    values_here = heads_here // GROUP
    w_full = lax.all_gather(w_out, "seq", axis=1, tiled=True)
    every_change = gather_seq(delta_v, nx, nz)
    every_change, cached_probs = lax.optimization_barrier((every_change, cached_probs))
    every_change = every_change.reshape(nx * nz * delta_v.shape[0] // BLK, BLK * values_here * HD)
    flat_lists = key_lists.reshape(blocks_here * topk_here)
    onehot = (flat_lists[:, None] == changed_block_numbers[None, :]).astype(jnp.bfloat16)
    selected = jnp.dot(onehot, every_change, preferred_element_type=jnp.float32)
    picked = selected.astype(jnp.bfloat16).reshape(blocks_here, topk_here, BLK, values_here * HD)
    attn_new = refresh(cached_probs, picked, out_old)
    n_head = w_full.shape[1] // attn_new.shape[1]
    w_groups = w_full.reshape(w_full.shape[0], n_head, attn_new.shape[1])
    terms = jnp.einsum("tk,kgc->gtc", attn_new, w_groups, preferred_element_type=jnp.float32)
    out_proj = lax.psum_scatter(terms.astype(jnp.bfloat16), "head", scatter_dimension=0, tiled=True)[0]
    return (attn_new, out_proj)


def solution(mesh):
    placed = (
        P("seq", "head", None, None, None),
        P("seq", "head"),
        P("seq", None),
        P(),
        P("seq", "head"),
        P("head", "seq"),
    )
    n_seq = mesh.shape["seq"]
    nz = 8 if n_seq % 8 == 0 else n_seq
    return jax.shard_map(
        lambda *a: local(n_seq // nz, nz, *a),
        mesh=mesh,
        in_specs=placed,
        out_specs=(P("seq", "head"), P("seq", "head")),
        check_vma=False,
    )
```

```python
import jax
import jax.numpy as jnp
from jax import lax
from jax.experimental import pallas as pl
from jax.experimental.pallas import tpu as pltpu
from jax.sharding import PartitionSpec as P

HD = 128
BLK = 128
GROUP = 5


def _gather_kernel(nx, nz, x_ref, o_ref, send1, recv1, send2, recv2, local_sem):
    me = lax.axis_index("seq")
    hh = lax.axis_index("head")
    mx = me // nz
    mz = lax.rem(me, nz)
    own = pltpu.make_async_copy(x_ref, o_ref.at[me], local_sem)
    own.start()
    first = []
    for k in range(1, nz):
        peer = mx * nz + lax.rem(mz + k, nz)
        copy = pltpu.make_async_remote_copy(
            src_ref=x_ref,
            dst_ref=o_ref.at[me],
            send_sem=send1.at[k],
            recv_sem=recv1.at[k],
            device_id=(peer, hh),
            device_id_type=pl.DeviceIdType.MESH,
        )
        copy.start()
        first.append(copy)
    own.wait()
    for copy in first:
        copy.wait_recv()
    row = pl.ds(pl.multiple_of(mx * nz, nz), nz)
    second = []
    for k in range(1, nx):
        peer = lax.rem(mx + k, nx) * nz + mz
        copy = pltpu.make_async_remote_copy(
            src_ref=o_ref.at[row],
            dst_ref=o_ref.at[row],
            send_sem=send2.at[k],
            recv_sem=recv2.at[k],
            device_id=(peer, hh),
            device_id_type=pl.DeviceIdType.MESH,
        )
        copy.start()
        second.append(copy)
    for copy in first:
        copy.wait_send()
    for copy in second:
        copy.wait_send()
    for copy in second:
        copy.wait_recv()


def gather_seq(x, nx, nz):
    n = nx * nz
    return pl.pallas_call(
        lambda *refs: _gather_kernel(nx, nz, *refs),
        out_shape=jax.ShapeDtypeStruct((n,) + x.shape, x.dtype),
        in_specs=[pl.BlockSpec(memory_space=pl.ANY)],
        out_specs=pl.BlockSpec(memory_space=pl.ANY),
        scratch_shapes=[
            pltpu.SemaphoreType.DMA((nz,)),
            pltpu.SemaphoreType.DMA((nz,)),
            pltpu.SemaphoreType.DMA((nx,)),
            pltpu.SemaphoreType.DMA((nx,)),
            pltpu.SemaphoreType.DMA,
        ],
        compiler_params=pltpu.CompilerParams(has_side_effects=True),
    )(x)


def _refresh_kernel(p_ref, v_ref, o_ref, out_ref, cols_ref):
    acc = o_ref[...].astype(jnp.float32)
    for k in range(p_ref.shape[2]):
        acc += jnp.dot(p_ref[0, 0, k], v_ref[0, k], preferred_element_type=jnp.float32)
    result = acc.astype(out_ref.dtype)
    out_ref[...] = result
    cols_ref[...] = result.T


def refresh(cached_probs, picked, out_old):
    blocks, heads, topk = cached_probs.shape[:3]
    return pl.pallas_call(
        _refresh_kernel,
        out_shape=(
            jax.ShapeDtypeStruct(out_old.shape, out_old.dtype),
            jax.ShapeDtypeStruct(out_old.shape[::-1], out_old.dtype),
        ),
        grid=(blocks, heads),
        in_specs=[
            pl.BlockSpec((1, 1, topk, BLK, BLK), lambda q, h: (q, h, 0, 0, 0)),
            pl.BlockSpec((1, topk, BLK, HD), lambda q, h: (q, 0, 0, h // GROUP)),
            pl.BlockSpec((BLK, HD), lambda q, h: (q, h)),
        ],
        out_specs=(
            pl.BlockSpec((BLK, HD), lambda q, h: (q, h)),
            pl.BlockSpec((HD, BLK), lambda q, h: (h, q)),
        ),
        cost_estimate=pl.CostEstimate(
            flops=2 * blocks * heads * topk * BLK * BLK * HD,
            bytes_accessed=2 * (cached_probs.size + picked.size + 2 * out_old.size),
            transcendentals=0,
        ),
    )(cached_probs, picked, out_old)


def local(nx, nz, cached_probs, out_old, key_lists, changed_block_numbers, delta_v, w_out):
    blocks_here = cached_probs.shape[0]
    heads_here = cached_probs.shape[1]
    topk_here = cached_probs.shape[2]
    values_here = heads_here // GROUP
    w_full = lax.all_gather(w_out, "seq", axis=1, tiled=True)
    every_change = gather_seq(delta_v, nx, nz)
    every_change, cached_probs = lax.optimization_barrier((every_change, cached_probs))
    every_change = every_change.reshape(nx * nz * delta_v.shape[0] // BLK, BLK * values_here * HD)
    flat_lists = key_lists.reshape(blocks_here * topk_here)
    onehot = (flat_lists[:, None] == changed_block_numbers[None, :]).astype(jnp.bfloat16)
    selected = jnp.dot(onehot, every_change, preferred_element_type=jnp.float32)
    picked = selected.astype(jnp.bfloat16).reshape(blocks_here, topk_here, BLK, values_here * HD)
    attn_new, attn_cols = refresh(cached_probs, picked, out_old)
    n_head = w_full.shape[1] // attn_new.shape[1]
    w_groups = w_full.reshape(w_full.shape[0], n_head, attn_new.shape[1])
    terms = jnp.einsum("kt,kgc->gtc", attn_cols, w_groups, preferred_element_type=jnp.float32)
    out_proj = lax.psum_scatter(terms.astype(jnp.bfloat16), "head", scatter_dimension=0, tiled=True)[0]
    return (attn_new, out_proj)


def solution(mesh):
    placed = (
        P("seq", "head", None, None, None),
        P("seq", "head"),
        P("seq", None),
        P(),
        P("seq", "head"),
        P("head", "seq"),
    )
    n_seq = mesh.shape["seq"]
    nz = 8 if n_seq % 8 == 0 else n_seq
    return jax.shard_map(
        lambda *a: local(n_seq // nz, nz, *a),
        mesh=mesh,
        in_specs=placed,
        out_specs=(P("seq", "head"), P("seq", "head")),
        check_vma=False,
    )
```

```python
import jax
import jax.numpy as jnp
from jax import lax
from jax.experimental import pallas as pl
from jax.experimental.pallas import tpu as pltpu
from jax.sharding import PartitionSpec as P

HD = 128
BLK = 128
GROUP = 5


def _gather_kernel(nx, nz, x_ref, o_ref, send1, recv1, send2, recv2, local_sem):
    me = lax.axis_index("seq")
    hh = lax.axis_index("head")
    mx = me // nz
    mz = lax.rem(me, nz)
    own = pltpu.make_async_copy(x_ref, o_ref.at[me], local_sem)
    own.start()
    first = []
    for k in range(1, nz):
        peer = mx * nz + lax.rem(mz + k, nz)
        copy = pltpu.make_async_remote_copy(
            src_ref=x_ref,
            dst_ref=o_ref.at[me],
            send_sem=send1.at[k],
            recv_sem=recv1.at[k],
            device_id=(peer, hh),
            device_id_type=pl.DeviceIdType.MESH,
        )
        copy.start()
        first.append(copy)
    own.wait()
    for copy in first:
        copy.wait_recv()
    row = pl.ds(pl.multiple_of(mx * nz, nz), nz)
    second = []
    for k in range(1, nx):
        peer = lax.rem(mx + k, nx) * nz + mz
        copy = pltpu.make_async_remote_copy(
            src_ref=o_ref.at[row],
            dst_ref=o_ref.at[row],
            send_sem=send2.at[k],
            recv_sem=recv2.at[k],
            device_id=(peer, hh),
            device_id_type=pl.DeviceIdType.MESH,
        )
        copy.start()
        second.append(copy)
    for copy in first:
        copy.wait_send()
    for copy in second:
        copy.wait_send()
    for copy in second:
        copy.wait_recv()


def gather_seq(x, nx, nz):
    n = nx * nz
    return pl.pallas_call(
        lambda *refs: _gather_kernel(nx, nz, *refs),
        out_shape=jax.ShapeDtypeStruct((n,) + x.shape, x.dtype),
        in_specs=[pl.BlockSpec(memory_space=pl.ANY)],
        out_specs=pl.BlockSpec(memory_space=pl.ANY),
        scratch_shapes=[
            pltpu.SemaphoreType.DMA((nz,)),
            pltpu.SemaphoreType.DMA((nz,)),
            pltpu.SemaphoreType.DMA((nx,)),
            pltpu.SemaphoreType.DMA((nx,)),
            pltpu.SemaphoreType.DMA,
        ],
        compiler_params=pltpu.CompilerParams(has_side_effects=True),
    )(x)


def local(nx, nz, cached_probs, out_old, key_lists, changed_block_numbers, delta_v, w_out):
    blocks_here = cached_probs.shape[0]
    heads_here = cached_probs.shape[1]
    topk_here = cached_probs.shape[2]
    values_here = heads_here // GROUP
    padded = jnp.pad(w_out, ((0, 8), (0, 0)))
    w_full = lax.all_gather(padded, "seq", axis=1, tiled=True)[:w_out.shape[0]]
    every_change = gather_seq(delta_v, nx, nz)
    every_change, cached_probs = lax.optimization_barrier((every_change, cached_probs))
    every_change = every_change.reshape(nx * nz * delta_v.shape[0] // BLK, BLK * values_here * HD)
    flat_lists = key_lists.reshape(blocks_here * topk_here)
    onehot = (flat_lists[:, None] == changed_block_numbers[None, :]).astype(jnp.bfloat16)
    selected = jnp.dot(onehot, every_change, preferred_element_type=jnp.float32)
    picked = selected.astype(jnp.bfloat16).reshape(blocks_here, topk_here, BLK, values_here, HD)
    tiles = cached_probs.reshape(blocks_here, values_here, GROUP, topk_here, BLK, BLK)
    delta_out = jnp.einsum("qvgkij,qkjvd->qivgd", tiles, picked, preferred_element_type=jnp.float32)
    delta_out = delta_out.reshape(blocks_here * BLK, heads_here * HD)
    attn_new = (out_old.astype(jnp.float32) + delta_out).astype(jnp.bfloat16)
    n_head = w_full.shape[1] // attn_new.shape[1]
    w_groups = w_full.reshape(w_full.shape[0], n_head, attn_new.shape[1])
    terms = jnp.einsum("tk,kgc->gtc", attn_new, w_groups, preferred_element_type=jnp.float32)
    out_proj = lax.psum_scatter(terms.astype(jnp.bfloat16), "head", scatter_dimension=0, tiled=True)[0]
    return (attn_new, out_proj)


def solution(mesh):
    placed = (
        P("seq", "head", None, None, None),
        P("seq", "head"),
        P("seq", None),
        P(),
        P("seq", "head"),
        P("head", "seq"),
    )
    n_seq = mesh.shape["seq"]
    nz = 8 if n_seq % 8 == 0 else n_seq
    return jax.shard_map(
        lambda *a: local(n_seq // nz, nz, *a),
        mesh=mesh,
        in_specs=placed,
        out_specs=(P("seq", "head"), P("seq", "head")),
        check_vma=False,
    )
```

```python
import jax
import jax.numpy as jnp
from jax import lax
from jax.experimental import pallas as pl
from jax.experimental.pallas import tpu as pltpu
from jax.sharding import PartitionSpec as P

HD = 128
BLK = 128
GROUP = 5


def _gather_kernel(nx, nz, x_ref, o_ref, send1, recv1, send2, recv2, local_sem):
    me = lax.axis_index("seq")
    hh = lax.axis_index("head")
    mx = me // nz
    mz = lax.rem(me, nz)
    own = pltpu.make_async_copy(x_ref, o_ref.at[me], local_sem)
    own.start()
    first = []
    for k in range(1, nz):
        peer = mx * nz + lax.rem(mz + k, nz)
        copy = pltpu.make_async_remote_copy(
            src_ref=x_ref,
            dst_ref=o_ref.at[me],
            send_sem=send1.at[k],
            recv_sem=recv1.at[k],
            device_id=(peer, hh),
            device_id_type=pl.DeviceIdType.MESH,
        )
        copy.start()
        first.append(copy)
    own.wait()
    for copy in first:
        copy.wait_recv()
    row = pl.ds(pl.multiple_of(mx * nz, nz), nz)
    second = []
    for k in range(1, nx):
        peer = lax.rem(mx + k, nx) * nz + mz
        copy = pltpu.make_async_remote_copy(
            src_ref=o_ref.at[row],
            dst_ref=o_ref.at[row],
            send_sem=send2.at[k],
            recv_sem=recv2.at[k],
            device_id=(peer, hh),
            device_id_type=pl.DeviceIdType.MESH,
        )
        copy.start()
        second.append(copy)
    for copy in first:
        copy.wait_send()
    for copy in second:
        copy.wait_send()
    for copy in second:
        copy.wait_recv()


def gather_seq(x, nx, nz):
    n = nx * nz
    return pl.pallas_call(
        lambda *refs: _gather_kernel(nx, nz, *refs),
        out_shape=jax.ShapeDtypeStruct((n,) + x.shape, x.dtype),
        in_specs=[pl.BlockSpec(memory_space=pl.ANY)],
        out_specs=pl.BlockSpec(memory_space=pl.ANY),
        scratch_shapes=[
            pltpu.SemaphoreType.DMA((nz,)),
            pltpu.SemaphoreType.DMA((nz,)),
            pltpu.SemaphoreType.DMA((nx,)),
            pltpu.SemaphoreType.DMA((nx,)),
            pltpu.SemaphoreType.DMA,
        ],
        compiler_params=pltpu.CompilerParams(has_side_effects=True),
    )(x)


def local(nx, nz, cached_probs, out_old, key_lists, changed_block_numbers, delta_v, w_out):
    blocks_here = cached_probs.shape[0]
    heads_here = cached_probs.shape[1]
    topk_here = cached_probs.shape[2]
    values_here = heads_here // GROUP
    w_full = lax.all_gather(w_out, "seq", axis=1, tiled=True)
    every_change = gather_seq(delta_v, nx, nz)
    every_change, cached_probs = lax.optimization_barrier((every_change, cached_probs))
    every_change = every_change.reshape(nx * nz * delta_v.shape[0] // BLK, BLK * values_here * HD)
    flat_lists = key_lists.reshape(blocks_here * topk_here)
    onehot = (flat_lists[:, None] == changed_block_numbers[None, :]).astype(jnp.bfloat16)
    selected = jnp.dot(onehot, every_change, preferred_element_type=jnp.float32)
    picked = selected.astype(jnp.bfloat16).reshape(blocks_here, topk_here, BLK, values_here, HD)
    tiles = cached_probs.reshape(blocks_here, values_here, GROUP, topk_here, BLK, BLK)
    delta_out = jnp.einsum("qvgkij,qkjvd->qivgd", tiles, picked, preferred_element_type=jnp.float32)
    delta_out = delta_out.reshape(blocks_here * BLK, heads_here * HD)
    attn_new = (out_old.astype(jnp.float32) + delta_out).astype(jnp.bfloat16)
    n_head = w_full.shape[1] // attn_new.shape[1]
    w_groups = w_full.reshape(w_full.shape[0], n_head, attn_new.shape[1])
    width = attn_new.shape[1]
    terms = jnp.stack([
        jnp.dot(attn_new, w_full[:, g * width:(g + 1) * width], preferred_element_type=jnp.float32).astype(jnp.bfloat16)
        for g in range(n_head)
    ])
    out_proj = lax.psum_scatter(terms, "head", scatter_dimension=0, tiled=True)[0]
    return (attn_new, out_proj)


def solution(mesh):
    placed = (
        P("seq", "head", None, None, None),
        P("seq", "head"),
        P("seq", None),
        P(),
        P("seq", "head"),
        P("head", "seq"),
    )
    n_seq = mesh.shape["seq"]
    nz = 8 if n_seq % 8 == 0 else n_seq
    return jax.shard_map(
        lambda *a: local(n_seq // nz, nz, *a),
        mesh=mesh,
        in_specs=placed,
        out_specs=(P("seq", "head"), P("seq", "head")),
        check_vma=False,
    )
```

```python
import jax
import jax.numpy as jnp
from jax import lax
from jax.experimental import pallas as pl
from jax.experimental.pallas import tpu as pltpu
from jax.sharding import PartitionSpec as P

HD = 128
BLK = 128
GROUP = 5


def _gather_kernel(nx, nz, x_ref, o_ref, send1, recv1, send2, recv2, local_sem):
    me = lax.axis_index("seq")
    hh = lax.axis_index("head")
    mx = me // nz
    mz = lax.rem(me, nz)
    own = pltpu.make_async_copy(x_ref, o_ref.at[me], local_sem)
    own.start()
    first = []
    for k in range(1, nz):
        peer = mx * nz + lax.rem(mz + k, nz)
        copy = pltpu.make_async_remote_copy(
            src_ref=x_ref,
            dst_ref=o_ref.at[me],
            send_sem=send1.at[k],
            recv_sem=recv1.at[k],
            device_id=(peer, hh),
            device_id_type=pl.DeviceIdType.MESH,
        )
        copy.start()
        first.append(copy)
    own.wait()
    for copy in first:
        copy.wait_recv()
    row = pl.ds(pl.multiple_of(mx * nz, nz), nz)
    second = []
    for k in range(1, nx):
        peer = lax.rem(mx + k, nx) * nz + mz
        copy = pltpu.make_async_remote_copy(
            src_ref=o_ref.at[row],
            dst_ref=o_ref.at[row],
            send_sem=send2.at[k],
            recv_sem=recv2.at[k],
            device_id=(peer, hh),
            device_id_type=pl.DeviceIdType.MESH,
        )
        copy.start()
        second.append(copy)
    for copy in first:
        copy.wait_send()
    for copy in second:
        copy.wait_send()
    for copy in second:
        copy.wait_recv()


def gather_seq(x, nx, nz):
    n = nx * nz
    return pl.pallas_call(
        lambda *refs: _gather_kernel(nx, nz, *refs),
        out_shape=jax.ShapeDtypeStruct((n,) + x.shape, x.dtype),
        in_specs=[pl.BlockSpec(memory_space=pl.ANY)],
        out_specs=pl.BlockSpec(memory_space=pl.ANY),
        scratch_shapes=[
            pltpu.SemaphoreType.DMA((nz,)),
            pltpu.SemaphoreType.DMA((nz,)),
            pltpu.SemaphoreType.DMA((nx,)),
            pltpu.SemaphoreType.DMA((nx,)),
            pltpu.SemaphoreType.DMA,
        ],
        compiler_params=pltpu.CompilerParams(has_side_effects=True),
    )(x)


def _project_kernel(chunks, a_ref, w_hbm, o_ref, w_vmem, sems):
    g = pl.program_id(0)
    width = a_ref.shape[1]
    rows = w_vmem.shape[0] // chunks
    per_chunk = rows // width

    def copy(i):
        part = pl.ds(i * rows, rows)
        return pltpu.make_async_copy(w_hbm.at[part], w_vmem.at[part], sems.at[i])

    @pl.when(g == 0)
    def _start():
        for i in range(chunks):
            copy(i).start()

    for i in range(chunks):
        pl.when(g == i * per_chunk)(lambda i=i: copy(i).wait())

    w = w_vmem[pl.ds(pl.multiple_of(g * width, width), width), :]
    term = lax.dot_general(a_ref[...], w, (((1,), (1,)), ((), ())), preferred_element_type=jnp.float32)
    o_ref[0] = term.astype(o_ref.dtype)


def project(a, w_t, chunks=4):
    rows, width = a.shape
    groups = w_t.shape[0] // width
    return pl.pallas_call(
        lambda *refs: _project_kernel(chunks, *refs),
        out_shape=jax.ShapeDtypeStruct((groups, rows, width), a.dtype),
        grid=(groups,),
        in_specs=[
            pl.BlockSpec((rows, width), lambda g: (0, 0)),
            pl.BlockSpec(memory_space=pl.ANY),
        ],
        out_specs=pl.BlockSpec((1, rows, width), lambda g: (g, 0, 0)),
        scratch_shapes=[
            pltpu.VMEM(w_t.shape, w_t.dtype),
            pltpu.SemaphoreType.DMA((chunks,)),
        ],
        cost_estimate=pl.CostEstimate(
            flops=2 * rows * width * w_t.shape[0],
            bytes_accessed=2 * (a.size + w_t.size + groups * rows * width),
            transcendentals=0,
        ),
    )(a, w_t)


def local(nx, nz, cached_probs, out_old, key_lists, changed_block_numbers, delta_v, w_out):
    blocks_here = cached_probs.shape[0]
    heads_here = cached_probs.shape[1]
    topk_here = cached_probs.shape[2]
    values_here = heads_here // GROUP
    w_full = lax.all_gather(w_out, "seq", axis=1, tiled=True)
    every_change = gather_seq(delta_v, nx, nz)
    every_change, cached_probs = lax.optimization_barrier((every_change, cached_probs))
    every_change = every_change.reshape(nx * nz * delta_v.shape[0] // BLK, BLK * values_here * HD)
    flat_lists = key_lists.reshape(blocks_here * topk_here)
    onehot = (flat_lists[:, None] == changed_block_numbers[None, :]).astype(jnp.bfloat16)
    selected = jnp.dot(onehot, every_change, preferred_element_type=jnp.float32)
    picked = selected.astype(jnp.bfloat16).reshape(blocks_here, topk_here, BLK, values_here, HD)
    tiles = cached_probs.reshape(blocks_here, values_here, GROUP, topk_here, BLK, BLK)
    delta_out = jnp.einsum("qvgkij,qkjvd->qivgd", tiles, picked, preferred_element_type=jnp.float32)
    delta_out = delta_out.reshape(blocks_here * BLK, heads_here * HD)
    attn_new = (out_old.astype(jnp.float32) + delta_out).astype(jnp.bfloat16)
    terms = project(attn_new, w_full.T)
    out_proj = lax.psum_scatter(terms, "head", scatter_dimension=0, tiled=True)[0]
    return (attn_new, out_proj)


def solution(mesh):
    placed = (
        P("seq", "head", None, None, None),
        P("seq", "head"),
        P("seq", None),
        P(),
        P("seq", "head"),
        P("head", "seq"),
    )
    n_seq = mesh.shape["seq"]
    nz = 8 if n_seq % 8 == 0 else n_seq
    return jax.shard_map(
        lambda *a: local(n_seq // nz, nz, *a),
        mesh=mesh,
        in_specs=placed,
        out_specs=(P("seq", "head"), P("seq", "head")),
        check_vma=False,
    )
```

```python
import jax
import jax.numpy as jnp
from jax import lax
from jax.experimental import pallas as pl
from jax.experimental.pallas import tpu as pltpu
from jax.sharding import PartitionSpec as P

HD = 128
BLK = 128
GROUP = 5


def _gather_kernel(nx, nz, x_ref, o_ref, send1, recv1, send2, recv2, local_sem):
    me = lax.axis_index("seq")
    hh = lax.axis_index("head")
    mx = me // nz
    mz = lax.rem(me, nz)
    own = pltpu.make_async_copy(x_ref, o_ref.at[me], local_sem)
    own.start()
    first = []
    for k in range(1, nz):
        peer = mx * nz + lax.rem(mz + k, nz)
        copy = pltpu.make_async_remote_copy(
            src_ref=x_ref,
            dst_ref=o_ref.at[me],
            send_sem=send1.at[k],
            recv_sem=recv1.at[k],
            device_id=(peer, hh),
            device_id_type=pl.DeviceIdType.MESH,
        )
        copy.start()
        first.append(copy)
    own.wait()
    for copy in first:
        copy.wait_recv()
    row = pl.ds(pl.multiple_of(mx * nz, nz), nz)
    second = []
    for k in range(1, nx):
        peer = lax.rem(mx + k, nx) * nz + mz
        copy = pltpu.make_async_remote_copy(
            src_ref=o_ref.at[row],
            dst_ref=o_ref.at[row],
            send_sem=send2.at[k],
            recv_sem=recv2.at[k],
            device_id=(peer, hh),
            device_id_type=pl.DeviceIdType.MESH,
        )
        copy.start()
        second.append(copy)
    for copy in first:
        copy.wait_send()
    for copy in second:
        copy.wait_send()
    for copy in second:
        copy.wait_recv()


def gather_seq(x, nx, nz):
    n = nx * nz
    return pl.pallas_call(
        lambda *refs: _gather_kernel(nx, nz, *refs),
        out_shape=jax.ShapeDtypeStruct((n,) + x.shape, x.dtype),
        in_specs=[pl.BlockSpec(memory_space=pl.ANY)],
        out_specs=pl.BlockSpec(memory_space=pl.ANY),
        scratch_shapes=[
            pltpu.SemaphoreType.DMA((nz,)),
            pltpu.SemaphoreType.DMA((nz,)),
            pltpu.SemaphoreType.DMA((nx,)),
            pltpu.SemaphoreType.DMA((nx,)),
            pltpu.SemaphoreType.DMA,
        ],
        compiler_params=pltpu.CompilerParams(has_side_effects=True),
    )(x)


def _refresh_kernel(p_ref, v_ref, o_ref, out_ref):
    acc = o_ref[...].astype(jnp.float32)
    for k in range(p_ref.shape[2]):
        acc += jnp.dot(p_ref[0, 0, k], v_ref[0, k], preferred_element_type=jnp.float32)
    out_ref[...] = acc.astype(out_ref.dtype)


def refresh(cached_probs, picked, out_old):
    blocks, heads, topk = cached_probs.shape[:3]
    return pl.pallas_call(
        _refresh_kernel,
        out_shape=jax.ShapeDtypeStruct(out_old.shape, jnp.float32),
        grid=(blocks, heads),
        in_specs=[
            pl.BlockSpec((1, 1, topk, BLK, BLK), lambda q, h: (q, h, 0, 0, 0)),
            pl.BlockSpec((1, topk, BLK, HD), lambda q, h: (q, 0, 0, h // GROUP)),
            pl.BlockSpec((BLK, HD), lambda q, h: (q, h)),
        ],
        out_specs=pl.BlockSpec((BLK, HD), lambda q, h: (q, h)),
        cost_estimate=pl.CostEstimate(
            flops=2 * blocks * heads * topk * BLK * BLK * HD,
            bytes_accessed=2 * (cached_probs.size + picked.size + 2 * out_old.size),
            transcendentals=0,
        ),
    )(cached_probs, picked, out_old)


def local(nx, nz, cached_probs, out_old, key_lists, changed_block_numbers, delta_v, w_out):
    blocks_here = cached_probs.shape[0]
    heads_here = cached_probs.shape[1]
    topk_here = cached_probs.shape[2]
    values_here = heads_here // GROUP
    w_full = lax.all_gather(w_out, "seq", axis=1, tiled=True)
    every_change = gather_seq(delta_v, nx, nz)
    every_change, cached_probs = lax.optimization_barrier((every_change, cached_probs))
    every_change = every_change.reshape(nx * nz * delta_v.shape[0] // BLK, BLK * values_here * HD)
    flat_lists = key_lists.reshape(blocks_here * topk_here)
    onehot = (flat_lists[:, None] == changed_block_numbers[None, :]).astype(jnp.bfloat16)
    selected = jnp.dot(onehot, every_change, preferred_element_type=jnp.float32)
    picked = selected.astype(jnp.bfloat16).reshape(blocks_here, topk_here, BLK, values_here * HD)
    attn_new = refresh(cached_probs, picked, out_old).astype(jnp.bfloat16)
    n_head = w_full.shape[1] // attn_new.shape[1]
    w_groups = w_full.reshape(w_full.shape[0], n_head, attn_new.shape[1])
    terms = jnp.einsum("tk,kgc->gtc", attn_new, w_groups, preferred_element_type=jnp.float32)
    out_proj = lax.psum_scatter(terms.astype(jnp.bfloat16), "head", scatter_dimension=0, tiled=True)[0]
    return (attn_new, out_proj)


def solution(mesh):
    placed = (
        P("seq", "head", None, None, None),
        P("seq", "head"),
        P("seq", None),
        P(),
        P("seq", "head"),
        P("head", "seq"),
    )
    n_seq = mesh.shape["seq"]
    nz = 8 if n_seq % 8 == 0 else n_seq
    return jax.shard_map(
        lambda *a: local(n_seq // nz, nz, *a),
        mesh=mesh,
        in_specs=placed,
        out_specs=(P("seq", "head"), P("seq", "head")),
        check_vma=False,
    )
```
